32 devices in a mesh: dp: 8 (over y, x, core), tensor: 4 (over z).
Axes of the slice: x: 2, y: 2, z: 4, core: 2. Of those that a mesh axis runs over, the one named last changes fastest.
Arguments:
- inputs: bfloat16 [12288, 4096], P('dp', 'tensor'), may hold values from -8 to 8
- cotangent: bfloat16 [12288, 14336], P('dp', 'tensor'), may hold values from -0.0546875 to 0.0546875
- sketch_basis: bfloat16 [14336, 256], P('tensor'), may hold values from -0.046875 to 0.046875
- first_moment: float32 [256, 14336], P('dp', 'tensor'), may hold values from -4 to 4
- second_moment: float32 [256, 14336], P('dp', 'tensor'), may hold values from 0.001 to 0.01
Outputs:
- basis: bfloat16 [4096, 256], P('tensor')
- new_first: float32 [256, 14336], P('dp', 'tensor')
- new_second: float32 [256, 14336], P('dp', 'tensor')
- update: float32 [4096, 14336], P('dp', 'tensor')
The draws below stay inside these ranges and needn't reach their ends.
All inputs are finite; a program needn't handle non-finite values.
Results may differ from the reference program's by a relative error of at most 0.03.
Values may be sent and summed in bfloat16 or wider, within the bound.
No kernel may reach another device: no remote copies, remote signals or barrier semaphores. Data moves between devices by JAX's collectives and lax.ppermute only.
A program may use at most 64 MiB of HBM per device.

```python
import math
import jax
import jax.numpy as jnp
from jax import lax

D = 4096
FF = 14336
RANK = 256
STEP = 10
TOKENS = 12288


def draw_inputs(key, part):
    first_key = jax.random.fold_in(jax.random.fold_in(key, 17), 0)
    values = jax.random.normal(first_key, (TOKENS, D), jnp.float32)
    return jnp.clip(values, -8.0, 8.0).astype(jnp.bfloat16)


def level_of(key, shape, shards, smallest, top_value):
    loudness, own = 1.0, jax.random.fold_in(key, 6)
    for dim, shards_of in shards:
        steps = jnp.exp(jax.random.uniform(jax.random.fold_in(own, dim), (shards_of,), jnp.float32, smallest / len(shards), top_value / len(shards)))
        loudness = loudness * jnp.repeat(steps, shape[dim] // shards_of).reshape([-1 if axis == dim else 1 for axis in range(len(shape))])
    return loudness


def bell_draw(key, shape, deviation, reach, cuts=(), dtype=jnp.bfloat16):
    drawn = jax.random.normal(key, shape, jnp.float32) * deviation
    if len(cuts) > 0:
        drawn = level_of(key, shape, cuts, -0.22, 0.18) * drawn
    return jnp.clip(drawn, min=-reach, max=reach).astype(dtype)


def setup_inputs(seed: int = 0) -> dict:
    key_list = jax.random.split(jax.random.key(seed), 6)
    inputs = draw_inputs(jax.random.fold_in(key_list[5], 71), 0)
    cotangent = bell_draw(key_list[1], (TOKENS, FF), TOKENS ** -0.5, 0.0546875, ((0, 8), (1, 4)))
    sketch_basis = bell_draw(key_list[2], (FF, RANK), FF ** -0.5, 0.046875, ((0, 4),))
    first_moment = bell_draw(key_list[3], (RANK, FF), 0.3, 4.0, ((0, 8), (1, 4)), jnp.float32)
    second_moment = jnp.clip(jnp.exp(math.log(0.01) - 2.30258502 * jax.random.uniform(key_list[4], (RANK, FF), jnp.float32) ** level_of(key_list[4], (RANK, FF), ((0, 8), (1, 4)), -0.2, 0.2)), 0.001, 0.01)
    return dict(inputs=inputs, cotangent=cotangent, sketch_basis=sketch_basis, first_moment=first_moment, second_moment=second_moment)


beta_first = 0.9
beta_second = 0.999
epsilon = 1e-08

def reference(inputs, cotangent, sketch_basis, first_moment, second_moment):
    token_sketch = jnp.dot(cotangent.astype(jnp.float32), sketch_basis.astype(jnp.float32), preferred_element_type=jnp.float32).astype(jnp.bfloat16)
    sketch = lax.dot_general(inputs.astype(jnp.float32), token_sketch.astype(jnp.float32), (((0,), (0,)), ((), ())), preferred_element_type=jnp.float32)
    gram = jnp.dot(sketch.T, sketch, precision=lax.Precision.HIGHEST)
    lower = jnp.linalg.cholesky(gram)
    basis_full = lax.linalg.triangular_solve(lower, sketch, left_side=False, lower=True, transpose_a=True)
    basis = basis_full.astype(jnp.bfloat16)
    reduced = jnp.dot(inputs.astype(jnp.float32), basis.astype(jnp.float32), preferred_element_type=jnp.float32).astype(jnp.bfloat16)
    projected = lax.dot_general(reduced.astype(jnp.float32), cotangent.astype(jnp.float32), (((0,), (0,)), ((), ())), preferred_element_type=jnp.float32)
    new_first = beta_first * first_moment + (1.0 - beta_first) * projected
    new_second = beta_second * second_moment + (1.0 - beta_second) * projected * projected
    fix_first = 1.0 - beta_first ** STEP
    fix_second = 1.0 - beta_second ** STEP
    direction = (new_first / fix_first / (jnp.sqrt(new_second / fix_second) + epsilon)).astype(jnp.bfloat16)
    update = jnp.dot(basis.astype(jnp.float32), direction.astype(jnp.float32), preferred_element_type=jnp.float32)
    return (basis, new_first, new_second, update)
```

```python
import functools

import jax
import jax.numpy as jnp
from jax import lax
from jax.experimental import pallas as pl
from jax.experimental.pallas import tpu as pltpu
from jax.sharding import PartitionSpec as P

STEP = 10

beta_first = 0.9
beta_second = 0.999
epsilon = 1e-08


BF = jnp.bfloat16
F32 = jnp.float32


def mm(a, b, ca, cb, precision=None):
    return lax.dot_general(
        a, b, (((ca,), (cb,)), ((), ())), precision=precision, preferred_element_type=F32
    )


def factor_block(m, b):
    ri = lax.broadcasted_iota(jnp.int32, (b, 1), 0)
    for j in range(0, b, 2):
        r0, r1 = m[j : j + 1, :], m[j + 1 : j + 2, :]
        c0, c1 = m[:, j : j + 1], m[:, j + 1 : j + 2]
        p00 = m[j : j + 1, j : j + 1]
        p01 = m[j : j + 1, j + 1 : j + 2]
        p11 = m[j + 1 : j + 2, j + 1 : j + 2]
        i0 = 1.0 / p00
        ratio = p01 * i0
        q11 = p11 - p01 * ratio
        i1 = 1.0 / q11
        r1 = r1 - ratio * r0
        c1 = c1 - ratio * c0
        k0 = jnp.where(ri > j + 1, c0 * i0, 0.0)
        k1 = jnp.where(ri > j + 1, c1 * i1, 0.0)
        rest = m - k0 * r0 - k1 * r1
        m = jnp.where(
            ri == j, r0 * lax.rsqrt(p00), jnp.where(ri == j + 1, r1 * lax.rsqrt(q11), rest)
        )
    return m


def inverse_factor_kernel(b, gram_ref, out_ref, aug):
    n = gram_ref.shape[0]
    hi_prec = lax.Precision.HIGHEST

    def eye(size):
        r = lax.broadcasted_iota(jnp.int32, (size, size), 0)
        return jnp.where(r == lax.broadcasted_iota(jnp.int32, (size, size), 1), 1.0, 0.0)

    aug[:, :n] = gram_ref[...]
    aug[:, n:] = eye(n)
    for k in range(n // b):
        lo, hi = k * b, (k + 1) * b
        m = factor_block(jnp.concatenate([aug[lo:hi, lo:hi], eye(b)], axis=1), b)
        rows = mm(m[:, b:], aug[lo:hi, :], 1, 0, hi_prec)
        out_ref[lo:hi, :] = rows[:, n:]
        if hi < n:
            aug[hi:, :] = aug[hi:, :] - mm(rows[:, hi:n], rows, 0, 0, hi_prec)


def inverse_factor(gram):
    n = gram.shape[0]
    return pl.pallas_call(
        functools.partial(inverse_factor_kernel, min(n, 128)),
        out_shape=jax.ShapeDtypeStruct((n, n), F32),
        in_specs=[pl.BlockSpec(memory_space=pltpu.VMEM)],
        out_specs=pl.BlockSpec(memory_space=pltpu.VMEM),
        scratch_shapes=[pltpu.VMEM((n, 2 * n), F32)],
        cost_estimate=pl.CostEstimate(
            flops=4 * n**3, bytes_accessed=8 * n * n, transcendentals=2 * n
        ),
        name="inverse_factor",
    )(gram)


def per_device(nd, nt, inputs, cotangent, sketch_basis, first_moment, second_moment):
    t, d = lax.axis_index("tensor"), lax.axis_index("dp")
    nq = nd // 2
    c, q = d % 2, d // 2
    tok, feat = inputs.shape
    rank = sketch_basis.shape[1]
    ct = tok // nt

    def rows(a, i, n):
        return lax.dynamic_slice_in_dim(a, i * n, n, 0)

    def tperm(x, k):
        return lax.ppermute(x, "tensor", [(i, i ^ k) for i in range(nt)])

    def qperm(x, k):
        return lax.ppermute(x, "dp", [(i, i ^ (2 * k)) for i in range(nd)])

    def cswap(x):
        return lax.ppermute(x, "dp", [(i, i ^ 1) for i in range(nd)])

    tks = sorted(range(1, nt), key=lambda k: (k < nt // 2, k))
    qks = sorted(range(1, nq), key=lambda k: (k < nq // 2, k))

    def put(pieces, index, n):
        total = jnp.zeros((n,) + pieces[0].shape, pieces[0].dtype)
        for k in range(n):
            total = lax.dynamic_update_index_in_dim(total, pieces[k], index ^ k, 0)
        return total

    def reduce_tokens(piece):
        got = {}
        for k in tks:
            got[k] = tperm(piece(k).astype(BF), k)
        own = piece(0)
        for k in tks:
            own = own + got[k].astype(F32)
        own = own.astype(BF)
        return put([own if k == 0 else tperm(own, k) for k in range(nt)], t, nt).reshape(tok, -1)

    def reduce_rows(keep, send):
        half = keep + cswap(send.astype(BF)).astype(F32)
        n = half.shape[0] // nq
        got = [qperm(rows(half, q ^ k, n).astype(BF), k) for k in qks]
        own = rows(half, q, n)
        for g in got:
            own = own + g.astype(F32)
        return own

    def gather_rows(own):
        half = put([own if k == 0 else qperm(own, k) for k in range(nq)], q, nq)
        return half, cswap(half)

    token_sketch = reduce_tokens(
        lambda k: jnp.dot(rows(cotangent, t ^ k, ct), sketch_basis, preferred_element_type=F32)
    )

    part = mm(inputs, token_sketch, 0, 0)
    own = reduce_rows(rows(part, c, feat // 2), rows(part, 1 - c, feat // 2)).astype(BF)
    half, other = gather_rows(own)
    half, other = half.reshape(feat // 2, rank), other.reshape(feat // 2, rank)
    first = c == 0
    sketch = jnp.concatenate(
        [jnp.where(first, half, other), jnp.where(first, other, half)], axis=0
    )

    rr = rank // nd
    share = rows(mm(sketch, sketch, 0, 0), d, rr)
    got = [tperm(share, k) for k in tks]
    for g in got:
        share = share + g
    half, other = gather_rows(share)
    gram = jnp.stack(
        [jnp.where(first, half, other), jnp.where(first, other, half)], axis=1
    ).reshape(rank, rank)
    factor = inverse_factor(gram)

    mixed = reduce_tokens(
        lambda k: jnp.dot(rows(inputs, t ^ k, ct), sketch, preferred_element_type=F32)
    )

    by_core = factor.reshape(nq, 2, rr, rank)
    ordered = jnp.concatenate(
        [
            lax.dynamic_index_in_dim(by_core, c, 1, keepdims=False).reshape(rank // 2, rank),
            lax.dynamic_index_in_dim(by_core, 1 - c, 1, keepdims=False).reshape(rank // 2, rank),
        ],
        axis=0,
    )

    def apply_factor(a, w):
        high = w.astype(BF)
        low = (w - high.astype(F32)).astype(BF)
        return (mm(a, high, 1, 1) + mm(a, low, 1, 1)).astype(BF)

    basis = apply_factor(sketch, factor)
    reduced = apply_factor(mixed, ordered)
    projected = reduce_rows(
        mm(reduced[:, : rank // 2], cotangent, 0, 0), mm(reduced[:, rank // 2 :], cotangent, 0, 0)
    )
    new_first = beta_first * first_moment + (1.0 - beta_first) * projected
    new_second = beta_second * second_moment + (1.0 - beta_second) * projected * projected
    fix_first = 1.0 - beta_first**STEP
    fix_second = 1.0 - beta_second**STEP
    direction = (new_first / fix_first / (jnp.sqrt(new_second / fix_second) + epsilon)).astype(BF)
    half, other = gather_rows(direction)
    direction = jnp.concatenate([half, other], axis=0).reshape(rank, -1)

    nrow = feat * nt // nd
    source, offset = d * nrow // feat, d * nrow % feat
    mine = lax.dynamic_slice_in_dim(sketch, offset, nrow, 0)
    row_sketch = jnp.where(t == source, mine, 0).astype(F32)
    for k in tks:
        pairs = []
        for i in range(nd):
            s = i * nrow // feat
            pairs.append((i * nt + s, i * nt + (s ^ k)))
        row_sketch = row_sketch + lax.ppermute(mine, ("dp", "tensor"), pairs).astype(F32)
    row_basis = apply_factor(row_sketch.astype(BF), ordered)
    update = jnp.dot(row_basis, direction, preferred_element_type=F32)
    return (basis, new_first, new_second, update)


def solution(mesh):
    return jax.shard_map(
        functools.partial(per_device, mesh.shape["dp"], mesh.shape["tensor"]),
        mesh=mesh,
        in_specs=(
            P("dp", "tensor"),
            P("dp", "tensor"),
            P("tensor", None),
            P("dp", "tensor"),
            P("dp", "tensor"),
        ),
        out_specs=(P("tensor", None), P("dp", "tensor"), P("dp", "tensor"), P("dp", "tensor")),
        check_vma=False,
    )
```

```python
import functools

import jax
import jax.numpy as jnp
from jax import lax
from jax.experimental import pallas as pl
from jax.experimental.pallas import tpu as pltpu
from jax.sharding import PartitionSpec as P

STEP = 10

beta_first = 0.9
beta_second = 0.999
epsilon = 1e-08


BF = jnp.bfloat16
F32 = jnp.float32
PARTS = 2
HIGHEST = lax.Precision.HIGHEST


def mm(a, b, ca, cb, precision=None):
    return lax.dot_general(
        a, b, (((ca,), (cb,)), ((), ())), precision=precision, preferred_element_type=F32
    )


def shape(dims, dtype):
    return jax.ShapeDtypeStruct(dims, dtype)


def cost(flops, moved):
    return pl.CostEstimate(flops=int(flops), bytes_accessed=int(moved), transcendentals=0)


def whole_call(kernel, outs, name, flops, *args, scratch=()):
    moved = sum(a.size * a.dtype.itemsize for a in args)
    vmem = pl.BlockSpec(memory_space=pltpu.VMEM)
    return pl.pallas_call(
        kernel,
        out_shape=outs,
        in_specs=[vmem] * len(args),
        out_specs=[vmem] * len(outs),
        scratch_shapes=list(scratch),
        cost_estimate=cost(flops, moved),
        name=name,
    )(*args)


def factor_block(m, b, panel):
    lanes = m.shape[1]
    groups = [m[8 * g : 8 * g + 8, :] for g in range(b // 8)]
    ri = lax.broadcasted_iota(jnp.int32, (8, lanes), 0)

    def wide(x):
        return jnp.broadcast_to(x, (8, lanes))

    for j0 in range(0, b, panel):
        first, at = j0 // 8, j0 % 8
        rest = range(first, b // 8)
        cols = [{g: wide(groups[g][:, j0 + i : j0 + i + 1]) for g in rest} for i in range(panel)]
        rows = [wide(groups[first][at + i : at + i + 1, :]) for i in range(panel)]
        block = {
            (i, k): wide(cols[k][first][at + i : at + i + 1, :])
            for i in range(panel)
            for k in range(i, panel)
        }
        for i in range(panel):
            scale = lax.rsqrt(block[i, i])
            rows[i] = rows[i] * scale
            below = {k: block[i, k] * scale for k in range(i + 1, panel)}
            for k in below:
                for f in range(k, panel):
                    block[k, f] = block[k, f] - below[k] * below[f]
                rows[k] = rows[k] - below[k] * rows[i]
            for g in rest:
                cols[i][g] = cols[i][g] * scale
                for k in below:
                    cols[k][g] = cols[k][g] - below[k] * cols[i][g]
        for g in rest:
            new = groups[g]
            for i in range(panel):
                new = new - cols[i][g] * rows[i]
            if g == first:
                new = jnp.where(ri >= at + panel, new, groups[g])
                for i in range(panel):
                    new = jnp.where(ri == at + i, rows[i], new)
            groups[g] = new
    return jnp.concatenate(groups, axis=0)


def identity(n):
    r = lax.broadcasted_iota(jnp.int32, (n, n), 0)
    return jnp.where(r == lax.broadcasted_iota(jnp.int32, (n, n), 1), 1.0, 0.0)


def split(w):
    high = w.astype(BF)
    return high, (w - high.astype(F32)).astype(BF)


def factor_kernel(nq, *refs):
    shares, (hi_ref, lo_ref, ohi_ref, olo_ref, aug, inv) = refs[:nq], refs[nq:]
    d = lax.axis_index("dp")
    q, c = d // 2, d % 2
    n = inv.shape[0]
    rr = n // (2 * nq)

    def group(k, parity):
        return pl.ds(pl.multiple_of((2 * (q ^ k) + parity) * rr, rr), rr)

    for k in range(nq):
        aug[group(k, c), :n] = shares[k][:rr, :]
        aug[group(k, 1 - c), :n] = shares[k][rr:, :]
    aug[:, n:] = identity(n)
    b = min(n, 64)
    for k in range(n // b):
        lo, hi = k * b, (k + 1) * b
        m = factor_block(jnp.concatenate([aug[lo:hi, lo:hi], identity(b)], axis=1), b, 8)
        rows = mm(m[:, b:], aug[lo:hi, :], 1, 0, HIGHEST)
        inv[lo:hi, :] = rows[:, n:]
        if hi < n:
            aug[hi:, :] = aug[hi:, :] - mm(rows[:, hi:n], rows, 0, 0, HIGHEST)
    hi_ref[...], lo_ref[...] = split(inv[...])
    for side, parity in enumerate((c, 1 - c)):
        for k in range(nq):
            at = (side * nq + k) * rr
            aug[at : at + rr, :n] = inv[group(k, parity), :]
    ohi_ref[...], olo_ref[...] = split(aug[:, :n])


def inverse_factor(shares):
    n = shares[0].shape[1]
    nq = len(shares)
    return whole_call(
        functools.partial(factor_kernel, nq),
        [shape((n, n), BF)] * 4,
        "inverse_factor",
        n * 128 * 128 * 160,
        *shares,
        scratch=[pltpu.VMEM((n, 2 * n), F32), pltpu.VMEM((n, n), F32)],
    )


def chunk_kernel(ks, base, a_ref, b_ref, *outs):
    i = pl.program_id(0)
    value = jnp.dot(a_ref[...], b_ref[...], preferred_element_type=F32).astype(BF)
    for j in range(ks):

        @pl.when(i == j)
        def _(j=j):
            outs[j][...] = value


def chunk_products(a, b, nt, base, ks, name):
    ct = a.shape[0] // nt
    rank = b.shape[1]
    t = lax.axis_index("tensor").astype(jnp.int32).reshape(1)
    grid_spec = pltpu.PrefetchScalarGridSpec(
        num_scalar_prefetch=1,
        grid=(ks,),
        in_specs=[
            pl.BlockSpec((ct, a.shape[1]), lambda i, t: (t[0] ^ (base + i), 0)),
            pl.BlockSpec(b.shape, lambda i, t: (0, 0)),
        ],
        out_specs=[pl.BlockSpec((ct, rank), lambda i, t: (0, 0))] * ks,
    )
    return pl.pallas_call(
        lambda t_ref, *refs: chunk_kernel(ks, base, *refs),
        grid_spec=grid_spec,
        out_shape=[shape((ct, rank), BF)] * ks,
        cost_estimate=cost(2 * ks * ct * a.shape[1] * rank, 2 * ks * ct * a.shape[1]),
        name=name,
    )(t, a, b)


def gram_kernel(h1, h2, o1, o2, sketch_ref, share_ref, gram):
    d = lax.axis_index("dp")
    c = d % 2
    n = h1.shape[0]

    def quarter(i):
        return pl.ds(pl.multiple_of(i * n, n), n)

    sketch_ref[quarter(2 * c), :] = h1[...]
    sketch_ref[quarter(2 * c + 1), :] = h2[...]
    sketch_ref[quarter(2 * (1 - c)), :] = o1[...]
    sketch_ref[quarter(2 * (1 - c) + 1), :] = o2[...]
    value = sketch_ref[...]
    gram[...] = mm(value, value, 0, 0)
    rr = share_ref.shape[0]
    share_ref[...] = gram[pl.ds(pl.multiple_of(d * rr, rr), rr), :]


def reduced_kernel(nt, *refs):
    chunks, (hi, lo, out_ref, laid) = refs[:nt], refs[nt:]
    t = lax.axis_index("tensor")
    ct = chunks[0].shape[0]
    for k in range(nt):
        laid[pl.ds(pl.multiple_of((t ^ k) * ct, ct), ct), :] = chunks[k][...]
    value = laid[...]
    out_ref[...] = (mm(hi[...], value, 1, 1) + mm(lo[...], value, 1, 1)).astype(BF)


def projected_kernel(r_ref, c_ref, keep_ref, send_ref):
    half = keep_ref.shape[0]
    value = jnp.dot(r_ref[...], c_ref[...], preferred_element_type=F32)
    keep_ref[...] = value[:half, :]
    send_ref[...] = value[half:, :].astype(BF)


def column_block(width):
    for lanes in (7, 8, 4, 2, 1):
        if width % (lanes * 128) == 0:
            return lanes * 128
    return width


def projected_part(reduced, cotangent, part, parts):
    rank, tok = reduced.shape
    width = cotangent.shape[1] // parts
    bn = column_block(width)
    nb = width // bn
    return pl.pallas_call(
        projected_kernel,
        grid=(nb,),
        in_specs=[
            pl.BlockSpec((rank, tok), lambda i: (0, 0)),
            pl.BlockSpec((tok, bn), lambda i: (0, part * nb + i)),
        ],
        out_specs=[pl.BlockSpec((rank // 2, bn), lambda i: (0, i))] * 2,
        out_shape=[shape((rank // 2, width), F32), shape((rank // 2, width), BF)],
        cost_estimate=cost(2 * rank * tok * width, 2 * tok * width),
        name=f"projected_{part}",
    )(reduced, cotangent)


def add_split_kernel(keep, got, own_ref, *outs):
    total = keep[...] + got[...].astype(F32)
    rr = own_ref.shape[0]
    own_ref[...] = total[:rr, :]
    for k, out in enumerate(outs, 1):
        out[...] = total[k * rr : (k + 1) * rr, :].astype(BF)


def adam_kernel(ng, *refs):
    own, got, (first, second), (new_first, new_second, direction) = (
        refs[0],
        refs[1 : 1 + ng],
        refs[1 + ng : 3 + ng],
        refs[-3:],
    )
    projected = own[...]
    for g in got:
        projected = projected + g[...].astype(F32)
    one = beta_first * first[...] + (1.0 - beta_first) * projected
    two = beta_second * second[...] + (1.0 - beta_second) * projected * projected
    new_first[...], new_second[...] = one, two
    fix_first = 1.0 - beta_first**STEP
    fix_second = 1.0 - beta_second**STEP
    direction[...] = (one / fix_first / (jnp.sqrt(two / fix_second) + epsilon)).astype(BF)


def adam_part(own, got, first, second, before, part):
    rr, width = own.shape
    here = pl.BlockSpec((rr, width), lambda i: (0, 0))
    mine = pl.BlockSpec((rr, width), lambda i: (0, part))
    ng = len(got)
    args = [own, *got, first, second]
    specs = [here] * (1 + ng) + [mine] * 2
    aliases = {}
    if before is not None:
        aliases = {len(args): 0, len(args) + 1: 1}
        args += list(before)
        specs += [pl.BlockSpec(memory_space=pl.ANY)] * 2
    return pl.pallas_call(
        functools.partial(adam_kernel, ng),
        grid=(1,),
        in_specs=specs,
        out_specs=[mine, mine, here],
        out_shape=[shape(first.shape, F32)] * 2 + [shape((rr, width), BF)],
        input_output_aliases=aliases,
        cost_estimate=cost(20 * rr * width, 24 * rr * width),
        name=f"adam_{part}",
    )(*args)


def update_kernel(np_, *refs):
    basis, pieces, out_ref = refs[0], refs[1 : 1 + np_], refs[-1]
    direction = jnp.concatenate([p[...] for p in pieces], axis=0)
    out_ref[...] = jnp.dot(basis[...], direction, preferred_element_type=F32)


def update_part(basis, pieces, before, ff, part):
    if pieces[0].shape[0] % 16:
        pieces = [jnp.concatenate(pieces, axis=0)]
    nrow, rank = basis.shape
    width = pieces[0].shape[1]
    bn = column_block(width)
    nb = width // bn
    args = [basis, *pieces]
    specs = [pl.BlockSpec((nrow, rank), lambda i: (0, 0))]
    specs += [pl.BlockSpec((p.shape[0], bn), lambda i: (0, i)) for p in pieces]
    aliases = {}
    if before is not None:
        aliases = {len(args): 0}
        args.append(before)
        specs.append(pl.BlockSpec(memory_space=pl.ANY))
    return pl.pallas_call(
        functools.partial(update_kernel, len(pieces)),
        grid=(nb,),
        in_specs=specs,
        out_specs=pl.BlockSpec((nrow, bn), lambda i: (0, part * nb + i)),
        out_shape=shape((nrow, ff), F32),
        input_output_aliases=aliases,
        cost_estimate=cost(2 * nrow * rank * width, 4 * nrow * width),
        name=f"update_{part}",
    )(*args)


def per_device(nd, nt, inputs, cotangent, sketch_basis, first_moment, second_moment):
    t, d = lax.axis_index("tensor"), lax.axis_index("dp")
    nq = nd // 2
    c = d % 2
    tok, feat = inputs.shape
    ff, rank = sketch_basis.shape
    ct = tok // nt

    def tperm(x, k):
        return lax.ppermute(x, "tensor", [(i, i ^ k) for i in range(nt)])

    def qperm(x, k):
        return lax.ppermute(x, "dp", [(i, i ^ (2 * k)) for i in range(nd)])

    def cswap(x):
        return lax.ppermute(x, "dp", [(i, i ^ 1) for i in range(nd)])

    tks = sorted(range(1, nt), key=lambda k: (k < nt // 2, k))
    qks = sorted(range(1, nq), key=lambda k: (k < nq // 2, k))

    def sum_chunks(chunks):
        got = {k: tperm(chunks[k], k) for k in tks}
        own = chunks[0].astype(F32)
        for k in tks:
            own = own + got[k].astype(F32)
        own = own.astype(BF)
        return [own if k == 0 else tperm(own, k) for k in range(nt)]

    far = chunk_products(cotangent, sketch_basis, nt, nt // 2, nt - nt // 2, "token_far")
    near = chunk_products(cotangent, sketch_basis, nt, 0, nt // 2, "token_near")
    chunks = sum_chunks([*near, *far])
    laid = jnp.zeros((nt, ct, rank), BF)
    for k in range(nt):
        laid = lax.dynamic_update_index_in_dim(laid, chunks[k], t ^ k, 0)
    token_sketch = laid.reshape(tok, rank)

    part = mm(inputs, token_sketch, 0, 0).astype(BF)
    swapped = cswap(part)
    n4 = feat // 4
    quarters = []
    for i in range(2):
        at = c * (2 * n4) + i * n4
        mine = lax.dynamic_slice_in_dim(part, at, n4, 0).astype(F32)
        theirs = lax.dynamic_slice_in_dim(swapped, at, n4, 0).astype(F32)
        quarters.append((mine + theirs).astype(BF))
    bits = [1 << b for b in range(nq.bit_length() - 1)]
    for one, two in zip(bits, reversed(bits)):
        got = [qperm(quarters[0], one), qperm(quarters[1], two)]
        quarters = [(a.astype(F32) + g.astype(F32)).astype(BF) for a, g in zip(quarters, got)]
    others = [cswap(a) for a in quarters]

    pairs = [
        ((2 * i + j) * nt + k, (2 * k + j) * nt + i)
        for i in range(nq)
        for j in range(2)
        for k in range(nt)
    ]
    row_sketch = lax.ppermute(jnp.concatenate(quarters, axis=0), ("dp", "tensor"), pairs)

    rr = rank // nd
    sketch, share = whole_call(
        gram_kernel,
        [shape((feat, rank), BF), shape((rr, rank), F32)],
        "gram",
        2 * feat * rank * rank,
        *quarters,
        *others,
        scratch=[pltpu.VMEM((rank, rank), F32)],
    )
    got = [tperm(share, k) for k in tks]
    for g in got:
        share = share + g
    share = jnp.concatenate([share, cswap(share)], axis=0)
    shares = [share if k == 0 else qperm(share, k) for k in range(nq)]
    high, low, own_high, own_low = inverse_factor(shares)

    mixed = sum_chunks(chunk_products(inputs, sketch, nt, 0, nt, "mixed"))
    (reduced,) = whole_call(
        functools.partial(reduced_kernel, nt),
        [shape((rank, tok), BF)],
        "reduced",
        4 * tok * rank * rank,
        *mixed,
        own_high,
        own_low,
        scratch=[pltpu.VMEM((tok, rank), BF)],
    )

    def apply_factor(a, hi, lo):
        return (mm(a, hi, 1, 1) + mm(a, lo, 1, 1)).astype(BF)

    basis = apply_factor(sketch, high, low)

    row_basis = apply_factor(row_sketch, own_high, own_low)

    parts = PARTS if (ff // PARTS) % 128 == 0 else 1
    moments, update = None, None
    for h in range(parts):
        keep, send = projected_part(reduced, cotangent, h, parts)
        got = cswap(send)
        width = ff // parts
        own, *away = whole_call(
            add_split_kernel,
            [shape((rr, width), F32)] + [shape((rr, width), BF)] * (nq - 1),
            f"add_{h}",
            rank * width,
            keep,
            got,
        )
        got = [qperm(away[k - 1], k) for k in qks]
        *moments, direction = adam_part(own, got, first_moment, second_moment, moments, h)
        pieces = [direction if k == 0 else qperm(direction, k) for k in range(nq)]
        pieces += [cswap(p) for p in pieces]
        update = update_part(row_basis, pieces, update, ff, h)
    return (basis, *moments, update)


def solution(mesh):
    return jax.shard_map(
        functools.partial(per_device, mesh.shape["dp"], mesh.shape["tensor"]),
        mesh=mesh,
        in_specs=(
            P("dp", "tensor"),
            P("dp", "tensor"),
            P("tensor", None),
            P("dp", "tensor"),
            P("dp", "tensor"),
        ),
        out_specs=(P("tensor", None), P("dp", "tensor"), P("dp", "tensor"), P("dp", "tensor")),
        check_vma=False,
    )
```
